512 devices in a mesh: dp: 8 (over y, core), expert: 64 (over x, z).
Axes of the slice: x: 4, y: 4, z: 16, core: 2. Of those that a mesh axis runs over, the one named last changes fastest.
Arguments:
- tokens: bfloat16 [4096, 2048], P('expert', 'dp'), may hold values from -6 to 6
- expert_ids: int32 [4096, 8], P('expert'), may hold values from 0 to 127, all different within a row; in each aligned block of 64 rows (0 to 63, 64 to 127, ...) at most 6 rows name the same one
- route_weights: bfloat16 [4096, 8], P('expert'), may hold values from 0.019897461 to 0.3984375
- w_gate: bfloat16 [128, 2048, 1024], P('expert', None, 'dp'), may hold values from -0.125 to 0.125
- w_up: bfloat16 [128, 2048, 1024], P('expert', None, 'dp'), may hold values from -0.125 to 0.125
- w_down: bfloat16 [128, 1024, 2048], P('expert', 'dp'), may hold values from -0.1875 to 0.1875
Outputs:
- moe_out: bfloat16 [4096, 2048], P('expert', 'dp')
The draws below stay inside these ranges and needn't reach their ends.
Inputs may be any that keep to these rules, and one draw needn't show every extreme that they name: `expert_ids`: each token names 8 different experts. In each aligned block of 64 rows no expert is named more than 6 times, a bound that some block reaches.
All inputs are finite; a program needn't handle non-finite values.
Results may differ from the reference program's by a relative error of at most 0.019.
Values may be sent and summed in bfloat16 or wider, within the bound.
A program may use at most 64 MiB of HBM per device.

```python
import math
import jax
import jax.numpy as jnp
import numpy as np
from jax import lax

D = 2048
FF = 1024
TOP_K = 8
TOK_DEV = 64
EXPERTS = 128
CAP = 6
TOKENS = 4096
N_DP = 8
N_EXPERT = 64


def shard_levels(own_key, extent, pieces, smallest, high):
    gain, own = 1.0, jax.random.fold_in(own_key, 6)
    for dim, blocks in pieces:
        draws = jnp.exp(jax.random.uniform(jax.random.fold_in(own, dim), (blocks,), jnp.float32, smallest / len(pieces), high / len(pieces)))
        gain = gain * jnp.repeat(draws, extent[dim] // blocks).reshape([-1 if axis == dim else 1 for axis in range(len(extent))])
    return gain


def shared_out(rng, own, number, rows, number_of, top, most, slope):
    ranking = jax.random.permutation(rng, number_of)
    packed, usual = shares(number_of, rows * top, most, slope, True), shares(number_of, rows * top, most, slope, False)
    places = jnp.arange(number_of)

    def named(lengths, turn):
        used = int((lengths > 0).sum())
        fixed = max(1, used // 4)
        moved = fixed + (places - fixed + turn * (used - fixed)) % max(1, number_of - fixed)
        return jnp.zeros((number_of,), jnp.int32).at[ranking[jnp.where(places < fixed, places, moved)]].set(jnp.asarray(lengths, jnp.int32))

    lengths = jnp.where(number % 4 == 0, named(packed, number // 4), named(usual, number - number // 4 - 1))
    mixed = jax.random.permutation(jax.random.fold_in(own, 3), number_of)
    giver, receiver = mixed[0:number_of // 2 * 2:2], mixed[1:number_of // 2 * 2:2]
    margin = jnp.minimum(lengths[giver] - 1, most - lengths[receiver]) // 2
    margin = jnp.where((giver == ranking[0]) | (receiver == ranking[0]) | (lengths[receiver] == 0), 0, jnp.maximum(margin, 0))
    moved = jax.random.randint(jax.random.fold_in(own, 4), (number_of // 2,), 0, 1 << 20) % (margin + 1)
    lengths = lengths.at[giver].add(-moved).at[receiver].add(moved)
    labels = jnp.searchsorted(jnp.cumsum(lengths), jnp.arange(rows * top), side="right").astype(jnp.int32)
    listing = labels.reshape(top, rows).T
    listing = listing[jax.random.permutation(jax.random.fold_in(own, 1), rows)]
    turn = jax.random.randint(jax.random.fold_in(own, 2), (rows, 1), 0, top)
    return jnp.take_along_axis(listing, (jnp.arange(top)[None, :] + turn) % top, axis=1)


def shares(count, total, reach, slope, full):
    weights = [(1 << 20) // math.isqrt(rank ** slope) + 1 for rank in range(1, count + 1)]
    largest = reach if full else min(reach, max(-(-total // count), total * weights[0] // sum(weights)))
    least = 1 if total - largest >= count - 1 else 0
    given, rest = [largest] + [least] * (count - 1), total - largest - least * (count - 1)
    while rest > 0:
        movable = [i for i in range(1, count) if given[i] < largest] or [i for i in range(1, count) if given[i] < reach]
        mass, left = sum([weights[i] for i in movable]), rest
        for i in movable:
            addition = min(reach - given[i], max(1, left * weights[i] // mass), rest)
            given[i] = given[i] + addition
            rest = rest - addition
    return np.array(given)


def centred(key, shape, width, reach, shards=(), kind=jnp.bfloat16):
    values = width * jax.random.normal(key, shape, jnp.float32)
    if shards:
        values = values * shard_levels(key, shape, shards, -0.22, 0.18)
    return jnp.clip(values, -reach, reach).astype(kind)


def setup_inputs(seed: int = 0) -> dict:
    splits = jax.random.split(jax.random.key(seed), 7)
    tokens = centred(splits[0], (TOKENS, D), 1.0, 6.0, ((0, 64), (1, 8)))
    expert_ids_keys = jax.random.split(jax.random.fold_in(splits[1], 1), TOKENS // TOK_DEV)
    expert_ids_turns = jax.random.permutation(jax.random.fold_in(splits[1], 3), TOKENS // TOK_DEV)
    expert_ids = jax.vmap(lambda own, number: shared_out(jax.random.fold_in(splits[1], 2), own, number, TOK_DEV, EXPERTS, TOP_K, CAP, 2))(expert_ids_keys, expert_ids_turns).reshape((TOKENS, TOP_K))
    route_weights = jnp.clip(jnp.exp(math.log(0.3984375) - 2.9969585 * jax.random.uniform(splits[2], (TOKENS, TOP_K), jnp.float32) ** shard_levels(splits[2], (TOKENS, TOP_K), ((0, 64),), -0.2, 0.2)), 0.019897461, 0.3984375).astype(jnp.bfloat16)
    w_gate = centred(splits[3], (EXPERTS, D, FF), D ** -0.5, 0.125, ((0, 64), (2, 8)))
    w_up = centred(splits[4], (EXPERTS, D, FF), D ** -0.5, 0.125, ((0, 64), (2, 8)))
    w_down = centred(splits[5], (EXPERTS, FF, D), FF ** -0.5, 0.1875, ((0, 64), (1, 8)))
    return {"tokens": tokens, "expert_ids": expert_ids, "route_weights": route_weights, "w_gate": w_gate, "w_up": w_up, "w_down": w_down}


def reference(tokens, expert_ids, route_weights, w_gate, w_up, w_down):
    flat_ids = expert_ids.reshape(-1).astype(jnp.int32)
    flat_weights = route_weights.reshape(-1).astype(jnp.float32)
    token_of = (jnp.arange(TOKENS * TOP_K, dtype=jnp.int32) // TOP_K).astype(jnp.int32)
    limit = N_EXPERT * CAP
    group_width = FF // N_DP

    def one_expert(total, expert_num):
        matches = flat_ids == expert_num
        picked = jnp.nonzero(matches, size=limit, fill_value=0)[0].astype(jnp.int32)
        live_rows = jnp.arange(limit, dtype=jnp.int32) < jnp.sum(matches.astype(jnp.int32))
        row_tokens = token_of[picked]
        rows = tokens[row_tokens]
        gate_proj = jnp.dot(rows, w_gate[expert_num], preferred_element_type=jnp.float32)
        up_proj = jnp.dot(rows, w_up[expert_num], preferred_element_type=jnp.float32)
        hidden = (jax.nn.silu(gate_proj) * up_proj).astype(jnp.bfloat16)
        hidden_groups = hidden.reshape(limit, N_DP, group_width).astype(jnp.float32)
        down_groups = w_down[expert_num].reshape(N_DP, group_width, D).astype(jnp.float32)
        partials = jnp.einsum("rgf,gfd->grd", hidden_groups, down_groups, precision=lax.Precision.HIGHEST)
        partials = lax.optimization_barrier(partials.astype(jnp.bfloat16)).astype(jnp.float32)
        scales = jnp.where(live_rows, flat_weights[picked], jnp.float32(0.0))
        terms = jnp.sum(partials * scales[None, :, None], axis=0)
        return total.at[row_tokens].add(terms), None

    start_total = jnp.zeros((TOKENS, D), jnp.float32)
    total, unused = lax.scan(one_expert, start_total, jnp.arange(EXPERTS, dtype=jnp.int32))
    return total.astype(jnp.bfloat16)
```

```python
import jax
import jax.numpy as jnp
from jax import lax
from jax.sharding import PartitionSpec as P


def slot_tables(expert_ids, route_weights, expert_count, capacity):
    flat_ids = expert_ids.reshape(-1)
    expert_range = jnp.arange(expert_count, dtype=jnp.int32)
    one_hot = (flat_ids[:, None] == expert_range[None, :]).astype(jnp.int32)
    ranks = jnp.sum((jnp.cumsum(one_hot, axis=0) - 1) * one_hot, axis=1)
    dest_slot = (flat_ids * capacity + ranks).reshape(expert_ids.shape)
    slot_range = jnp.arange(expert_count * capacity, dtype=jnp.int32)
    hit_table = dest_slot[None, :, :] == slot_range[:, None, None]
    dispatch_matrix = jnp.sum(hit_table.astype(jnp.float32), axis=2).astype(jnp.bfloat16)
    weight_table = jnp.where(
        hit_table, route_weights.astype(jnp.float32)[None, :, :], jnp.float32(0.0)
    )
    combine_matrix = jnp.sum(weight_table, axis=2).astype(jnp.bfloat16)
    return (dispatch_matrix, combine_matrix)


def on_device(tokens, expert_ids, route_weights, w_gate, w_up, w_down):
    peer_count = lax.axis_size("expert")
    dp_count = lax.axis_size("dp")
    local_experts, width, group = w_gate.shape
    expert_count = local_experts * peer_count
    tok_rows, top_count = expert_ids.shape
    feats = tokens.shape[1]
    capacity = tok_rows * top_count * 3 // (2 * expert_count)
    dispatch_matrix, combine_matrix = slot_tables(expert_ids, route_weights, expert_count, capacity)
    send_rows = jnp.dot(dispatch_matrix, tokens, preferred_element_type=jnp.float32).astype(
        jnp.bfloat16
    )
    send_rows = send_rows.reshape(peer_count, local_experts * capacity, feats)
    arrived = lax.all_to_all(send_rows, "expert", split_axis=0, concat_axis=0, tiled=True)
    arrived = arrived.reshape(peer_count, local_experts, capacity, feats).transpose(1, 0, 2, 3)
    arrived = arrived.reshape(local_experts, peer_count * capacity, feats)
    whole = lax.all_gather(arrived, "dp", axis=0)
    w_gate = w_gate.reshape(local_experts, dp_count, feats, group)
    w_up = w_up.reshape(local_experts, dp_count, feats, group)
    gate_proj = jnp.einsum("grnd,rgdf->rnf", whole, w_gate, preferred_element_type=jnp.float32)
    up_proj = jnp.einsum("grnd,rgdf->rnf", whole, w_up, preferred_element_type=jnp.float32)
    hidden = (jax.nn.silu(gate_proj) * up_proj).astype(jnp.bfloat16)
    partial = jnp.einsum("rnf,rfd->rnd", hidden, w_down, preferred_element_type=jnp.float32)
    partial = partial.astype(jnp.bfloat16).reshape(local_experts * peer_count * capacity, width)
    summed = lax.psum_scatter(partial, "dp", scatter_dimension=1, tiled=True)
    summed = summed.reshape(local_experts, peer_count, capacity, feats).transpose(1, 0, 2, 3)
    summed = summed.reshape(peer_count, local_experts * capacity, feats)
    returned = lax.all_to_all(summed, "expert", split_axis=0, concat_axis=0, tiled=True)
    flat_returned = returned.reshape(expert_count * capacity, feats)
    return lax.dot_general(
        combine_matrix, flat_returned, (((0,), (0,)), ((), ())), preferred_element_type=jnp.float32
    ).astype(jnp.bfloat16)


def solution(mesh):
    return jax.shard_map(
        on_device,
        mesh=mesh,
        in_specs=(
            P("expert", "dp"),
            P("expert", None),
            P("expert", None),
            P("expert", None, "dp"),
            P("expert", None, "dp"),
            P("expert", "dp", None),
        ),
        out_specs=P("expert", "dp"),
        check_vma=False,
    )
```

```python
import functools

import jax
import jax.numpy as jnp
from jax import lax
from jax.experimental import pallas as pl
from jax.experimental.pallas import tpu as pltpu
from jax.sharding import PartitionSpec as P

MESH = pl.DeviceIdType.MESH
NX, NY, NZ = 4, 4, 16
CAP = 6
SLOT = NX * 2 * CAP
GROUPS = 4
PER = NZ // GROUPS
GROWS = PER * SLOT
HALF = GROWS // 2


def kernel(
    tok_ref, ids_ref, rw_ref, wg_ref, wu_ref, wd_ref, out_ref,
    tx, meta, send, gath, wgu, wdn, comb, psib, own, sib, uni, hl, hr, fl, fr, fin, ret, acc, xout, xin,
    x_ss, x_rs, m_ss, m_rs, z_ss, z_rs, ag_ss, ag_rs, rs_ss, rs_rs, zr_ss, zr_rs, xr_ss, xr_rs, w_sem,
):
    f32, bf16 = jnp.float32, jnp.bfloat16
    rows_n, feats = tok_ref.shape
    d, ex = lax.axis_index("dp"), lax.axis_index("expert")
    y, c = d // 2, d % 2
    x, z = ex // NZ, ex % NZ
    yr, yl, yo = (y + 1) % NY, (y + NY - 1) % NY, (y + 2) % NY
    right, left, sibling = (yr * 2 + c, ex), (yl * 2 + c, ex), (y * 2 + 1 - c, ex)

    def xpeer(i):
        return (d, ((x + i) % NX) * NZ + z)

    def zpeer(o):
        return (d, x * NZ + (z + o) % NZ)

    def offset(s):
        return (s + 1) // 2 if s % 2 else (NZ - s // 2) % NZ

    def remote(src, dst, ss, rs, dev):
        return pltpu.make_async_remote_copy(
            src_ref=src, dst_ref=dst, send_sem=ss, recv_sem=rs, device_id=dev, device_id_type=MESH
        )

    sent = []

    def go(src, dst, ss, rs, dev):
        copy = remote(src, dst, ss, rs, dev)
        copy.start()
        sent.append(copy)

    def arrive(dst, ss, rs, dev):
        remote(dst, dst, ss, rs, dev).wait_recv()

    barrier = pltpu.get_barrier_semaphore()
    partners = [xpeer(i) for i in range(1, NX)] + [zpeer(o) for o in range(1, NZ)] + [right, left, sibling]
    for dev in partners:
        pl.semaphore_signal(barrier, inc=1, device_id=dev, device_id_type=MESH)

    weights = [
        pltpu.make_async_copy(wg_ref.at[0], wgu.at[:, 0:128], w_sem.at[0]),
        pltpu.make_async_copy(wg_ref.at[1], wgu.at[:, 128:256], w_sem.at[1]),
        pltpu.make_async_copy(wu_ref.at[0], wgu.at[:, 256:384], w_sem.at[2]),
        pltpu.make_async_copy(wu_ref.at[1], wgu.at[:, 384:512], w_sem.at[3]),
        pltpu.make_async_copy(wd_ref.at[0], wdn.at[0:128, :], w_sem.at[4]),
        pltpu.make_async_copy(wd_ref.at[1], wdn.at[128:256, :], w_sem.at[5]),
    ]
    for copy in weights:
        copy.start()

    meta[x] = jnp.zeros((16, 128), f32)
    meta[x, 0:8, 0:64] = ids_ref[...].astype(f32)
    meta[x, 8:16, 0:64] = rw_ref[...].astype(f32)
    tx[x] = tok_ref[...]
    acc[...] = jnp.zeros(acc.shape, f32)
    pl.semaphore_wait(barrier, len(partners))

    for i in range(1, NX):
        go(meta.at[x], meta.at[x], m_ss.at[i], m_rs.at[i], xpeer(i))
    for i in range(1, NX):
        go(tok_ref, tx.at[x], x_ss.at[i], x_rs.at[i], xpeer(i))

    shape = (NZ * 8, NX * rows_n)
    q = lax.broadcasted_iota(jnp.int32, shape, 0)
    t = lax.broadcasted_iota(jnp.int32, shape, 1)
    s = q >> 3
    off = jnp.where((s & 1) == 1, (s + 1) >> 1, (NZ - (s >> 1)) & (NZ - 1))
    expert = 2 * (x * NZ + ((z + off) & (NZ - 1))) + (q & 1)
    expert = jnp.where(((q >> 1) & (NX - 1)) == (t >> 6), expert, -1).astype(f32)
    t0 = lax.broadcasted_iota(jnp.int32, (NX * rows_n, NX * rows_n), 0)
    t1 = lax.broadcasted_iota(jnp.int32, (NX * rows_n, NX * rows_n), 1)
    before = jnp.where((t0 < t1) & ((t0 >> 6) == (t1 >> 6)), f32(1), f32(0)).astype(bf16)
    low = lax.broadcasted_iota(jnp.int32, (16, 128), 1) < 64

    for i in range(1, NX):
        arrive(meta.at[(x + NX - i) % NX], m_ss.at[i], m_rs.at[i], xpeer(i))
    info = jnp.concatenate(
        [jnp.where(low, meta[b], pltpu.roll(meta[b + 1], 64, 1)) for b in (0, 2)], axis=1
    )
    named = jnp.zeros(shape, f32)
    scale = jnp.zeros(shape, f32)
    for k in range(8):
        hit = info[k : k + 1, :] == expert
        named = named + jnp.where(hit, f32(1), f32(0))
        scale = scale + jnp.where(hit, info[8 + k : 9 + k, :], f32(0))
    rank = jnp.dot(named.astype(bf16), before, preferred_element_type=f32)
    rank = jnp.where(named > 0, rank, f32(-1)).reshape(NZ, 1, 8, NX * rows_n)
    place = lax.broadcasted_iota(jnp.int32, (NZ, CAP, 8, NX * rows_n), 1).astype(f32)
    chosen = jnp.broadcast_to(rank, place.shape) == place
    pick = jnp.where(chosen, f32(1), f32(0)).reshape(NZ * SLOT, NX * rows_n).astype(bf16)
    for i in range(1, NX):
        arrive(tx.at[(x + NX - i) % NX], x_ss.at[i], x_rs.at[i], xpeer(i))
    rows = jnp.dot(pick, tx[...].reshape(NX * rows_n, feats), preferred_element_type=f32).astype(bf16)
    send[...] = rows
    for s in range(1, NZ):
        part = pl.ds(s * SLOT, SLOT)
        go(send.at[part, :], gath.at[d, part, :], z_ss.at[s], z_rs.at[s], zpeer(offset(s)))
    gath[d, 0:SLOT, :] = rows[0:SLOT, :]
    scale = jnp.broadcast_to(scale.reshape(NZ, 1, 8, NX * rows_n), place.shape)
    mix = jnp.where(chosen, scale, f32(0)).reshape(NZ * SLOT, NX * rows_n)
    comb[...] = mix.astype(bf16)

    def group(g):
        return pl.ds(g * GROWS, GROWS)

    def first(g):
        return pl.ds(g * GROWS, HALF)

    def second(g):
        return pl.ds(g * GROWS + HALF, HALF)

    def step_own(g):
        for s in range(max(1, g * PER), (g + 1) * PER):
            arrive(gath.at[d, pl.ds(s * SLOT, SLOT), :], z_ss.at[s], z_rs.at[s], zpeer(offset(s)))
        mine = gath.at[d, group(g), :]
        go(mine, mine, ag_ss.at[g, 0], ag_rs.at[g, 0], right)
        go(mine, mine, ag_ss.at[g, 1], ag_rs.at[g, 1], left)
        go(mine, mine, ag_ss.at[g, 2], ag_rs.at[g, 2], sibling)

    def step_forward(g):
        from_l, from_r = yl * 2 + c, yr * 2 + c
        arrive(gath.at[from_l, group(g), :], ag_ss.at[g, 0], ag_rs.at[g, 0], right)
        part = gath.at[from_l, first(g), :]
        go(part, part, ag_ss.at[g, 3], ag_rs.at[g, 3], right)
        arrive(gath.at[from_r, group(g), :], ag_ss.at[g, 1], ag_rs.at[g, 1], left)
        part = gath.at[from_r, second(g), :]
        go(part, part, ag_ss.at[g, 4], ag_rs.at[g, 4], left)
        part = gath.at[from_l, group(g), :]
        go(part, part, ag_ss.at[g, 5], ag_rs.at[g, 5], sibling)
        part = gath.at[from_r, group(g), :]
        go(part, part, ag_ss.at[g, 6], ag_rs.at[g, 6], sibling)

    def step_last(g):
        far = yo * 2 + c
        arrive(gath.at[far, first(g), :], ag_ss.at[g, 3], ag_rs.at[g, 3], right)
        arrive(gath.at[far, second(g), :], ag_ss.at[g, 4], ag_rs.at[g, 4], left)
        part = gath.at[far, group(g), :]
        go(part, part, ag_ss.at[g, 7], ag_rs.at[g, 7], sibling)

    def step_experts(g):
        for i, yy in ((2, y), (5, yl), (6, yr), (7, yo)):
            arrive(gath.at[yy * 2 + 1 - c, group(g), :], ag_ss.at[g, i], ag_rs.at[g, i], sibling)
        if g == 0:
            for copy in weights:
                copy.wait()
        lhs = jnp.concatenate([gath[i, group(g), :] for i in range(2 * NY)], axis=1)
        both = jnp.dot(lhs, wgu[...], preferred_element_type=f32)
        gate, up = both[:, 0:256], both[:, 256:512]
        hidden = gate / (f32(1) + jnp.exp(-gate)) * up
        r = lax.broadcasted_iota(jnp.int32, hidden.shape, 0)
        lane = lax.broadcasted_iota(jnp.int32, hidden.shape, 1)
        hidden = jnp.where((r & 1) == (lane >> 7), hidden, f32(0)).astype(bf16)
        for yy in range(NY):
            cols = pl.ds(pl.multiple_of((2 * yy + 1 - c) * feats, feats), feats)
            psib[yy, group(g), :] = jnp.dot(hidden, wdn[:, cols], preferred_element_type=f32).astype(bf16)
        go(psib.at[:, group(g), :], sib.at[:, group(g), :], rs_ss.at[g, 0], rs_rs.at[g, 0], sibling)
        for yy in range(NY):
            cols = pl.ds(pl.multiple_of((2 * yy + c) * feats, feats), feats)
            own[yy, group(g), :] = jnp.dot(hidden, wdn[:, cols], preferred_element_type=f32)

    def step_pair(g):
        arrive(sib.at[:, group(g), :], rs_ss.at[g, 0], rs_rs.at[g, 0], sibling)
        for yy in range(NY):
            total = own[yy, group(g), :] + sib[yy, group(g), :].astype(f32)
            uni[yy, group(g), :] = total.astype(bf16)
        into = pl.ds(g * HALF, HALF)
        go(uni.at[yo, first(g), :], hl.at[into, :], rs_ss.at[g, 1], rs_rs.at[g, 1], right)
        go(uni.at[yo, second(g), :], hr.at[into, :], rs_ss.at[g, 2], rs_rs.at[g, 2], left)

    def step_near(g):
        into = pl.ds(g * HALF, HALF)
        arrive(hl.at[into, :], rs_ss.at[g, 1], rs_rs.at[g, 1], right)
        total = uni[yr, first(g), :].astype(f32) + hl[into, :].astype(f32)
        uni[yr, first(g), :] = total.astype(bf16)
        go(uni.at[yr, group(g), :], fl.at[group(g), :], rs_ss.at[g, 3], rs_rs.at[g, 3], right)
        arrive(hr.at[into, :], rs_ss.at[g, 2], rs_rs.at[g, 2], left)
        total = uni[yl, second(g), :].astype(f32) + hr[into, :].astype(f32)
        uni[yl, second(g), :] = total.astype(bf16)
        go(uni.at[yl, group(g), :], fr.at[group(g), :], rs_ss.at[g, 4], rs_rs.at[g, 4], left)

    def step_back(g):
        arrive(fl.at[group(g), :], rs_ss.at[g, 3], rs_rs.at[g, 3], right)
        arrive(fr.at[group(g), :], rs_ss.at[g, 4], rs_rs.at[g, 4], left)
        total = uni[y, group(g), :].astype(f32) + fl[group(g), :].astype(f32) + fr[group(g), :].astype(f32)
        total = total.astype(bf16)
        fin[group(g), :] = total
        for s in range(max(1, g * PER), (g + 1) * PER):
            part = pl.ds(s * SLOT, SLOT)
            go(fin.at[part, :], ret.at[part, :], zr_ss.at[s], zr_rs.at[s], zpeer(NZ - offset(s)))
        if g == 0:
            ret[0:SLOT, :] = total[0:SLOT, :]

    def step_mix(g):
        for s in range(max(1, g * PER), (g + 1) * PER):
            part = pl.ds(s * SLOT, SLOT)
            arrive(ret.at[part, :], zr_ss.at[s], zr_rs.at[s], zpeer(NZ - offset(s)))
        acc[...] += lax.dot_general(
            comb[group(g), :], ret[group(g), :], (((0,), (0,)), ((), ())), preferred_element_type=f32
        )

    steps = [step_own, step_forward, step_last, step_experts, step_pair, step_near, step_back, step_mix]
    for tick in range(GROUPS + len(steps) - 1):
        for k in reversed(range(len(steps))):
            if 0 <= tick - k < GROUPS:
                steps[k](tick - k)

    xout[...] = acc[...].astype(bf16).reshape(NX, rows_n, feats)
    for i in range(1, NX):
        go(xout.at[(x + i) % NX], xin.at[i], xr_ss.at[i], xr_rs.at[i], xpeer(i))
    total = acc[pl.ds(pl.multiple_of(x * rows_n, rows_n), rows_n), :]
    for i in range(1, NX):
        arrive(xin.at[i], xr_ss.at[i], xr_rs.at[i], xpeer(i))
        total = total + xin[i].astype(f32)
    out_ref[...] = total.astype(bf16)
    for copy in sent:
        copy.wait_send()


def on_device(tokens, expert_ids, route_weights, w_gate, w_up, w_down):
    rows_n, feats = tokens.shape
    vm, dma = pltpu.VMEM, pltpu.SemaphoreType.DMA
    bf16, f32 = jnp.bfloat16, jnp.float32
    total = NZ * SLOT
    width = w_gate.shape[1]
    in_vmem = pl.BlockSpec(memory_space=pltpu.VMEM)
    in_any = pl.BlockSpec(memory_space=pl.ANY)
    return pl.pallas_call(
        kernel,
        out_shape=jax.ShapeDtypeStruct((rows_n, feats), bf16),
        in_specs=[in_vmem] * 3 + [in_any] * 3,
        out_specs=in_vmem,
        scratch_shapes=[
            vm((NX, rows_n, feats), bf16),
            vm((NX, 16, 128), f32),
            vm((total, feats), bf16),
            vm((2 * NY, total, feats), bf16),
            vm((width, 512), bf16),
            vm((256, width), bf16),
            vm((total, NX * rows_n), bf16),
            vm((NY, total, feats), bf16),
            vm((NY, total, feats), f32),
            vm((NY, total, feats), bf16),
            vm((NY, total, feats), bf16),
            vm((total // 2, feats), bf16),
            vm((total // 2, feats), bf16),
            vm((total, feats), bf16),
            vm((total, feats), bf16),
            vm((total, feats), bf16),
            vm((total, feats), bf16),
            vm((NX * rows_n, feats), f32),
            vm((NX, rows_n, feats), bf16),
            vm((NX, rows_n, feats), bf16),
            dma((NX,)), dma((NX,)), dma((NX,)), dma((NX,)),
            dma((NZ,)), dma((NZ,)),
            dma((GROUPS, 8)), dma((GROUPS, 8)),
            dma((GROUPS, 5)), dma((GROUPS, 5)),
            dma((NZ,)), dma((NZ,)),
            dma((NX,)), dma((NX,)),
            dma((6,)),
        ],
        compiler_params=pltpu.CompilerParams(
            collective_id=0, has_side_effects=True, vmem_limit_bytes=40 << 20
        ),
    )(tokens, expert_ids.T, route_weights.T, w_gate, w_up, w_down)


def solution(mesh):
    return jax.shard_map(
        on_device,
        mesh=mesh,
        in_specs=(
            P("expert", "dp"),
            P("expert", None),
            P("expert", None),
            P("expert", None, "dp"),
            P("expert", None, "dp"),
            P("expert", "dp", None),
        ),
        out_specs=P("expert", "dp"),
        check_vma=False,
    )
```

```python
import functools

import jax
import jax.numpy as jnp
from jax import lax
from jax.experimental import pallas as pl
from jax.experimental.pallas import tpu as pltpu
from jax.sharding import PartitionSpec as P

MESH = pl.DeviceIdType.MESH
NX, NY, NZ = 4, 4, 16
CAP = 6
SLOT = NX * 2 * CAP
GROUPS = 4
PER = NZ // GROUPS
GROWS = PER * SLOT
HALF = GROWS // 2
OFFSETS = (0, 8, 4, 12, 1, 9, 5, 13, 2, 10, 6, 14, 3, 11, 7, 15)
AHEAD = 2
ORDER = (
    (0, 0), (1, 0), (0, 1), (2, 0), (3, 0), (0, 2), (1, 1), (4, 0),
    (1, 2), (0, 3), (2, 1), (5, 0), (3, 1), (2, 2), (4, 1), (1, 3),
    (3, 2), (6, 0), (5, 1), (4, 2), (2, 3), (3, 3), (6, 1), (5, 2),
    (4, 3), (6, 2), (5, 3), (6, 3), (7, 0), (7, 1), (7, 2), (7, 3),
)


def kernel(
    tok_ref, ids_ref, rw_ref, wg_ref, wu_ref, wd_ref, out_ref,
    tx, ids_v, rw_v, meta, send, gath, wgu, wdn, comb, psib, own, sib, uni, hl, hr, fl, fr, fin, ret, acc, xout, xin,
    x_ss, x_rs, m_ss, m_rs, z_ss, z_rs, ag_ss, ag_rs, rs_ss, rs_rs, zr_ss, zr_rs, xr_ss, xr_rs, w_sem,
):
    f32, bf16 = jnp.float32, jnp.bfloat16
    rows_n, feats = tok_ref.shape
    d, ex = lax.axis_index("dp"), lax.axis_index("expert")
    y, c = d // 2, d % 2
    x, z = ex // NZ, ex % NZ
    yr, yl, yo = (y + 1) % NY, (y + NY - 1) % NY, (y + 2) % NY
    right, left, sibling = (yr * 2 + c, ex), (yl * 2 + c, ex), (y * 2 + 1 - c, ex)

    def xpeer(i):
        return (d, ((x + i) % NX) * NZ + z)

    def zpeer(o):
        return (d, x * NZ + (z + o) % NZ)

    def offset(s):
        return OFFSETS[s]

    def remote(src, dst, ss, rs, dev):
        return pltpu.make_async_remote_copy(
            src_ref=src, dst_ref=dst, send_sem=ss, recv_sem=rs, device_id=dev, device_id_type=MESH
        )

    sent = []

    def go(src, dst, ss, rs, dev):
        copy = remote(src, dst, ss, rs, dev)
        copy.start()
        sent.append(copy)

    def arrive(dst, ss, rs, dev):
        remote(dst, dst, ss, rs, dev).wait_recv()

    barrier = pltpu.get_barrier_semaphore()
    partners = [xpeer(i) for i in range(1, NX)] + [zpeer(o) for o in range(1, NZ)] + [right, left, sibling]
    for dev in partners:
        pl.semaphore_signal(barrier, inc=1, device_id=dev, device_id_type=MESH)

    x_in = [
        pltpu.make_async_copy(ids_ref, ids_v, w_sem.at[6]),
        pltpu.make_async_copy(rw_ref, rw_v, w_sem.at[7]),
        pltpu.make_async_copy(tok_ref, tx.at[x], w_sem.at[8]),
    ]
    for copy in x_in:
        copy.start()
    weights = [
        pltpu.make_async_copy(wg_ref.at[0], wgu.at[:, 0:128], w_sem.at[0]),
        pltpu.make_async_copy(wg_ref.at[1], wgu.at[:, 128:256], w_sem.at[1]),
        pltpu.make_async_copy(wu_ref.at[0], wgu.at[:, 256:384], w_sem.at[2]),
        pltpu.make_async_copy(wu_ref.at[1], wgu.at[:, 384:512], w_sem.at[3]),
        pltpu.make_async_copy(wd_ref.at[0], wdn.at[0:128, :], w_sem.at[4]),
        pltpu.make_async_copy(wd_ref.at[1], wdn.at[128:256, :], w_sem.at[5]),
    ]
    for copy in weights:
        copy.start()

    meta[x] = jnp.zeros((16, 128), f32)
    acc[...] = jnp.zeros(acc.shape, f32)
    for copy in x_in:
        copy.wait()
    meta[x, 0:8, 0:64] = ids_v[...].astype(f32)
    meta[x, 8:16, 0:64] = rw_v[...].astype(f32)
    pl.semaphore_wait(barrier, len(partners))

    for i in range(1, NX):
        go(meta.at[x], meta.at[x], m_ss.at[i], m_rs.at[i], xpeer(i))
    for i in range(1, NX):
        go(tx.at[x], tx.at[x], x_ss.at[i], x_rs.at[i], xpeer(i))

    shape = (NZ * 8, NX * rows_n)
    q = lax.broadcasted_iota(jnp.int32, shape, 0)
    t = lax.broadcasted_iota(jnp.int32, shape, 1)
    s = q >> 3
    off = (s >> 2) + ((s & 2) << 1) + ((s & 1) << 3)
    expert = 2 * (x * NZ + ((z + off) & (NZ - 1))) + (q & 1)
    expert = jnp.where(((q >> 1) & (NX - 1)) == (t >> 6), expert, -1).astype(f32)
    t0 = lax.broadcasted_iota(jnp.int32, (NX * rows_n, NX * rows_n), 0)
    t1 = lax.broadcasted_iota(jnp.int32, (NX * rows_n, NX * rows_n), 1)
    before = jnp.where((t0 < t1) & ((t0 >> 6) == (t1 >> 6)), f32(1), f32(0)).astype(bf16)
    low = lax.broadcasted_iota(jnp.int32, (16, 128), 1) < 64

    for i in range(1, NX):
        arrive(meta.at[(x + NX - i) % NX], m_ss.at[i], m_rs.at[i], xpeer(i))
    info = jnp.concatenate(
        [jnp.where(low, meta[b], pltpu.roll(meta[b + 1], 64, 1)) for b in (0, 2)], axis=1
    )
    named = jnp.zeros(shape, f32)
    scale = jnp.zeros(shape, f32)
    for k in range(8):
        hit = info[k : k + 1, :] == expert
        named = named + jnp.where(hit, f32(1), f32(0))
        scale = scale + jnp.where(hit, info[8 + k : 9 + k, :], f32(0))
    rank = jnp.dot(named.astype(bf16), before, preferred_element_type=f32)
    rank = jnp.where(named > 0, rank, f32(-1)).reshape(NZ, 1, 8, NX * rows_n)
    place = lax.broadcasted_iota(jnp.int32, (NZ, CAP, 8, NX * rows_n), 1).astype(f32)
    chosen = jnp.broadcast_to(rank, place.shape) == place
    pick = jnp.where(chosen, f32(1), f32(0)).reshape(NZ * SLOT, NX * rows_n).astype(bf16)
    for i in range(1, NX):
        arrive(tx.at[(x + NX - i) % NX], x_ss.at[i], x_rs.at[i], xpeer(i))
    rows = jnp.dot(pick, tx[...].reshape(NX * rows_n, feats), preferred_element_type=f32).astype(bf16)
    send[...] = rows

    def step_out(g):
        for s in range(max(1, g * PER), (g + 1) * PER):
            part = pl.ds(s * SLOT, SLOT)
            go(send.at[part, :], gath.at[d, part, :], z_ss.at[s], z_rs.at[s], zpeer(offset(s)))

    for g in range(AHEAD):
        step_out(g)
    gath[d, 0:SLOT, :] = rows[0:SLOT, :]
    scale = jnp.broadcast_to(scale.reshape(NZ, 1, 8, NX * rows_n), place.shape)
    mix = jnp.where(chosen, scale, f32(0)).reshape(NZ * SLOT, NX * rows_n)
    comb[...] = mix.astype(bf16)

    def group(g):
        return pl.ds(g * GROWS, GROWS)

    def first(g):
        return pl.ds(g * GROWS, HALF)

    def second(g):
        return pl.ds(g * GROWS + HALF, HALF)

    def step_own(g):
        for s in range(max(1, g * PER), (g + 1) * PER):
            arrive(gath.at[d, pl.ds(s * SLOT, SLOT), :], z_ss.at[s], z_rs.at[s], zpeer(offset(s)))
        if g + AHEAD < GROUPS:
            step_out(g + AHEAD)
        mine = gath.at[d, group(g), :]
        go(mine, mine, ag_ss.at[g, 0], ag_rs.at[g, 0], right)
        go(mine, mine, ag_ss.at[g, 1], ag_rs.at[g, 1], left)
        go(mine, mine, ag_ss.at[g, 2], ag_rs.at[g, 2], sibling)

    def step_forward(g):
        from_l, from_r = yl * 2 + c, yr * 2 + c
        arrive(gath.at[from_l, group(g), :], ag_ss.at[g, 0], ag_rs.at[g, 0], right)
        part = gath.at[from_l, first(g), :]
        go(part, part, ag_ss.at[g, 3], ag_rs.at[g, 3], right)
        arrive(gath.at[from_r, group(g), :], ag_ss.at[g, 1], ag_rs.at[g, 1], left)
        part = gath.at[from_r, second(g), :]
        go(part, part, ag_ss.at[g, 4], ag_rs.at[g, 4], left)
        part = gath.at[from_l, group(g), :]
        go(part, part, ag_ss.at[g, 5], ag_rs.at[g, 5], sibling)
        part = gath.at[from_r, group(g), :]
        go(part, part, ag_ss.at[g, 6], ag_rs.at[g, 6], sibling)

    def step_last(g):
        far = yo * 2 + c
        arrive(gath.at[far, first(g), :], ag_ss.at[g, 3], ag_rs.at[g, 3], right)
        arrive(gath.at[far, second(g), :], ag_ss.at[g, 4], ag_rs.at[g, 4], left)
        part = gath.at[far, group(g), :]
        go(part, part, ag_ss.at[g, 7], ag_rs.at[g, 7], sibling)

    def step_experts(g):
        for i, yy in ((2, y), (5, yl), (6, yr), (7, yo)):
            arrive(gath.at[yy * 2 + 1 - c, group(g), :], ag_ss.at[g, i], ag_rs.at[g, i], sibling)
        if g == 0:
            for copy in weights:
                copy.wait()
        lhs = jnp.concatenate([gath[i, group(g), :] for i in range(2 * NY)], axis=1)
        both = jnp.dot(lhs, wgu[...], preferred_element_type=f32)
        gate, up = both[:, 0:256], both[:, 256:512]
        hidden = gate / (f32(1) + jnp.exp(-gate)) * up
        r = lax.broadcasted_iota(jnp.int32, hidden.shape, 0)
        lane = lax.broadcasted_iota(jnp.int32, hidden.shape, 1)
        hidden = jnp.where((r & 1) == (lane >> 7), hidden, f32(0)).astype(bf16)
        for yy in range(NY):
            cols = pl.ds(pl.multiple_of((2 * yy + 1 - c) * feats, feats), feats)
            psib[yy, group(g), :] = jnp.dot(hidden, wdn[:, cols], preferred_element_type=f32).astype(bf16)
        go(psib.at[:, group(g), :], sib.at[:, group(g), :], rs_ss.at[g, 0], rs_rs.at[g, 0], sibling)
        for yy in range(NY):
            cols = pl.ds(pl.multiple_of((2 * yy + c) * feats, feats), feats)
            own[yy, group(g), :] = jnp.dot(hidden, wdn[:, cols], preferred_element_type=f32)

    def step_pair(g):
        arrive(sib.at[:, group(g), :], rs_ss.at[g, 0], rs_rs.at[g, 0], sibling)
        for yy in range(NY):
            total = own[yy, group(g), :] + sib[yy, group(g), :].astype(f32)
            uni[yy, group(g), :] = total.astype(bf16)
        into = pl.ds(g * HALF, HALF)
        go(uni.at[yo, first(g), :], hl.at[into, :], rs_ss.at[g, 1], rs_rs.at[g, 1], right)
        go(uni.at[yo, second(g), :], hr.at[into, :], rs_ss.at[g, 2], rs_rs.at[g, 2], left)

    def step_near(g):
        into = pl.ds(g * HALF, HALF)
        arrive(hl.at[into, :], rs_ss.at[g, 1], rs_rs.at[g, 1], right)
        total = uni[yr, first(g), :].astype(f32) + hl[into, :].astype(f32)
        uni[yr, first(g), :] = total.astype(bf16)
        go(uni.at[yr, group(g), :], fl.at[group(g), :], rs_ss.at[g, 3], rs_rs.at[g, 3], right)
        arrive(hr.at[into, :], rs_ss.at[g, 2], rs_rs.at[g, 2], left)
        total = uni[yl, second(g), :].astype(f32) + hr[into, :].astype(f32)
        uni[yl, second(g), :] = total.astype(bf16)
        go(uni.at[yl, group(g), :], fr.at[group(g), :], rs_ss.at[g, 4], rs_rs.at[g, 4], left)

    def step_back(g):
        arrive(fl.at[group(g), :], rs_ss.at[g, 3], rs_rs.at[g, 3], right)
        arrive(fr.at[group(g), :], rs_ss.at[g, 4], rs_rs.at[g, 4], left)
        total = uni[y, group(g), :].astype(f32) + fl[group(g), :].astype(f32) + fr[group(g), :].astype(f32)
        total = total.astype(bf16)
        fin[group(g), :] = total
        for s in range(max(1, g * PER), (g + 1) * PER):
            part = pl.ds(s * SLOT, SLOT)
            go(fin.at[part, :], ret.at[part, :], zr_ss.at[s], zr_rs.at[s], zpeer(NZ - offset(s)))
        if g == 0:
            ret[0:SLOT, :] = total[0:SLOT, :]

    def step_mix(g):
        for s in range(max(1, g * PER), (g + 1) * PER):
            part = pl.ds(s * SLOT, SLOT)
            arrive(ret.at[part, :], zr_ss.at[s], zr_rs.at[s], zpeer(NZ - offset(s)))
        acc[...] += lax.dot_general(
            comb[group(g), :], ret[group(g), :], (((0,), (0,)), ((), ())), preferred_element_type=f32
        )

    steps = [step_own, step_forward, step_last, step_experts, step_pair, step_near, step_back, step_mix]
    for k, g in ORDER:
        steps[k](g)

    xout[...] = acc[...].astype(bf16).reshape(NX, rows_n, feats)
    for i in range(1, NX):
        go(xout.at[(x + i) % NX], xin.at[i], xr_ss.at[i], xr_rs.at[i], xpeer(i))
    total = acc[pl.ds(pl.multiple_of(x * rows_n, rows_n), rows_n), :]
    for i in range(1, NX):
        arrive(xin.at[i], xr_ss.at[i], xr_rs.at[i], xpeer(i))
        total = total + xin[i].astype(f32)
    out_ref[...] = total.astype(bf16)
    for copy in sent:
        copy.wait_send()


def on_device(tokens, expert_ids, route_weights, w_gate, w_up, w_down):
    rows_n, feats = tokens.shape
    vm, dma = pltpu.VMEM, pltpu.SemaphoreType.DMA
    bf16, f32 = jnp.bfloat16, jnp.float32
    total = NZ * SLOT
    width = w_gate.shape[1]
    in_vmem = pl.BlockSpec(memory_space=pltpu.VMEM)
    in_hbm = pl.BlockSpec(memory_space=pltpu.HBM)
    return pl.pallas_call(
        kernel,
        out_shape=jax.ShapeDtypeStruct((rows_n, feats), bf16),
        in_specs=[in_hbm] * 6,
        out_specs=in_vmem,
        scratch_shapes=[
            vm((NX, rows_n, feats), bf16),
            vm((8, rows_n), jnp.int32),
            vm((8, rows_n), bf16),
            vm((NX, 16, 128), f32),
            vm((total, feats), bf16),
            vm((2 * NY, total, feats), bf16),
            vm((width, 512), bf16),
            vm((256, width), bf16),
            vm((total, NX * rows_n), bf16),
            vm((NY, total, feats), bf16),
            vm((NY, total, feats), f32),
            vm((NY, total, feats), bf16),
            vm((NY, total, feats), bf16),
            vm((total // 2, feats), bf16),
            vm((total // 2, feats), bf16),
            vm((total, feats), bf16),
            vm((total, feats), bf16),
            vm((total, feats), bf16),
            vm((total, feats), bf16),
            vm((NX * rows_n, feats), f32),
            vm((NX, rows_n, feats), bf16),
            vm((NX, rows_n, feats), bf16),
            dma((NX,)), dma((NX,)), dma((NX,)), dma((NX,)),
            dma((NZ,)), dma((NZ,)),
            dma((GROUPS, 8)), dma((GROUPS, 8)),
            dma((GROUPS, 5)), dma((GROUPS, 5)),
            dma((NZ,)), dma((NZ,)),
            dma((NX,)), dma((NX,)),
            dma((9,)),
        ],
        compiler_params=pltpu.CompilerParams(
            collective_id=0, has_side_effects=True, vmem_limit_bytes=60 << 20
        ),
    )(tokens, expert_ids.T, route_weights.T, w_gate, w_up, w_down)


def solution(mesh):
    return jax.shard_map(
        on_device,
        mesh=mesh,
        in_specs=(
            P("expert", "dp"),
            P("expert", None),
            P("expert", None),
            P("expert", None, "dp"),
            P("expert", None, "dp"),
            P("expert", "dp", None),
        ),
        out_specs=P("expert", "dp"),
        check_vma=False,
    )
```

```python
import functools

import jax
import jax.numpy as jnp
from jax import lax
from jax.experimental import pallas as pl
from jax.experimental.pallas import tpu as pltpu
from jax.sharding import PartitionSpec as P

MESH = pl.DeviceIdType.MESH
NX, NY, NZ = 4, 4, 16
CAP = 6
SLOT = NX * 2 * CAP
GROUPS = 7
STARTS = (0, 2, 4, 6, 8, 10, 12, 16)
OFFSETS = (6, 10, 5, 11, 0, 8, 3, 13, 4, 12, 7, 9, 2, 14, 1, 15)
DIRECT = (True, False, False, False, False, True, False)
OWN = 4
AHEAD = 6
ORDER = (
    (0, 0), (0, 1), (1, 0), (0, 3), (2, 0), (1, 1), (0, 2), (3, 0),
    (0, 4), (4, 0), (5, 0), (1, 3), (2, 1), (1, 2), (3, 1), (1, 4),
    (4, 1), (0, 6), (0, 5), (2, 3), (6, 0), (2, 2), (2, 4), (3, 3),
    (5, 1), (3, 2), (3, 4), (4, 3), (4, 2), (1, 6), (4, 4), (1, 5),
    (2, 5), (6, 1), (5, 3), (3, 5), (5, 2), (2, 6), (4, 5), (5, 5),
    (5, 4), (3, 6), (6, 3), (6, 2), (4, 6), (6, 5), (6, 4), (5, 6),
    (6, 6), (7, 0), (7, 1), (7, 3), (7, 2), (7, 5), (7, 4), (7, 6),
)


def kernel(
    tok_ref, ids_ref, rw_ref, wg_ref, wu_ref, wd_ref, out_ref,
    tx, ids_v, rw_v, meta, send, gath, wgu, wdn, comb, psib, own, sib, uni, far, fl, fr, fin, ret, acc, xout, xin,
    x_ss, x_rs, m_ss, m_rs, z_ss, z_rs, ag_ss, ag_rs, rs_ss, rs_rs, zr_ss, zr_rs, xr_ss, xr_rs, w_sem,
):
    f32, bf16 = jnp.float32, jnp.bfloat16
    rows_n, feats = tok_ref.shape
    d, ex = lax.axis_index("dp"), lax.axis_index("expert")
    y, c = d // 2, d % 2
    x, z = ex // NZ, ex % NZ
    yr, yl, yo = (y + 1) % NY, (y + NY - 1) % NY, (y + 2) % NY
    right, left, across = (yr * 2 + c, ex), (yl * 2 + c, ex), (yo * 2 + c, ex)
    sibling = (y * 2 + 1 - c, ex)

    def xpeer(i):
        return (d, ((x + i) % NX) * NZ + z)

    def zpeer(o):
        return (d, x * NZ + (z + o) % NZ)

    def offset(s):
        return OFFSETS[s]

    def remote(src, dst, ss, rs, dev):
        return pltpu.make_async_remote_copy(
            src_ref=src, dst_ref=dst, send_sem=ss, recv_sem=rs, device_id=dev, device_id_type=MESH
        )

    sent, ready = [], []

    def go(src, dst, ss, rs, dev):
        copy = remote(src, dst, ss, rs, dev)
        copy.start()
        sent.append(copy)

    def arrive(dst, ss, rs, dev):
        remote(dst, dst, ss, rs, dev).wait_recv()

    def group(g):
        return pl.ds(STARTS[g] * SLOT, (STARTS[g + 1] - STARTS[g]) * SLOT)

    barrier = pltpu.get_barrier_semaphore()
    partners = [xpeer(i) for i in range(1, NX)] + [zpeer(o) for o in range(1, NZ)] + [right, left, across, sibling]
    for dev in partners:
        pl.semaphore_signal(barrier, inc=1, device_id=dev, device_id_type=MESH)

    x_in = [
        pltpu.make_async_copy(ids_ref, ids_v, w_sem.at[6]),
        pltpu.make_async_copy(rw_ref, rw_v, w_sem.at[7]),
        pltpu.make_async_copy(tok_ref, tx.at[x], w_sem.at[8]),
    ]
    for copy in x_in:
        copy.start()
    weights = [
        pltpu.make_async_copy(wg_ref.at[0], wgu.at[:, 0:128], w_sem.at[0]),
        pltpu.make_async_copy(wg_ref.at[1], wgu.at[:, 128:256], w_sem.at[1]),
        pltpu.make_async_copy(wu_ref.at[0], wgu.at[:, 256:384], w_sem.at[2]),
        pltpu.make_async_copy(wu_ref.at[1], wgu.at[:, 384:512], w_sem.at[3]),
        pltpu.make_async_copy(wd_ref.at[0], wdn.at[0:128, :], w_sem.at[4]),
        pltpu.make_async_copy(wd_ref.at[1], wdn.at[128:256, :], w_sem.at[5]),
    ]
    for copy in weights:
        copy.start()

    meta[x] = jnp.zeros((16, 128), f32)
    acc[...] = jnp.zeros(acc.shape, f32)
    for copy in x_in:
        copy.wait()
    meta[x, 0:8, 0:64] = ids_v[...].astype(f32)
    meta[x, 8:16, 0:64] = rw_v[...].astype(f32)
    pl.semaphore_wait(barrier, len(partners))

    for i in range(1, NX):
        go(meta.at[x], meta.at[x], m_ss.at[i], m_rs.at[i], xpeer(i))
    for i in range(1, NX):
        go(tx.at[x], tx.at[x], x_ss.at[i], x_rs.at[i], xpeer(i))

    shape = (NZ * 8, NX * rows_n)
    q = lax.broadcasted_iota(jnp.int32, shape, 0)
    t = lax.broadcasted_iota(jnp.int32, shape, 1)
    s = q >> 3
    off = jnp.zeros(shape, jnp.int32)
    for i in range(NZ):
        off = jnp.where(s == i, OFFSETS[i], off)
    expert = 2 * (x * NZ + ((z + off) & (NZ - 1))) + (q & 1)
    expert = jnp.where(((q >> 1) & (NX - 1)) == (t >> 6), expert, -1).astype(f32)
    t0 = lax.broadcasted_iota(jnp.int32, (NX * rows_n, NX * rows_n), 0)
    t1 = lax.broadcasted_iota(jnp.int32, (NX * rows_n, NX * rows_n), 1)
    before = jnp.where((t0 < t1) & ((t0 >> 6) == (t1 >> 6)), f32(1), f32(0)).astype(bf16)
    low = lax.broadcasted_iota(jnp.int32, (16, 128), 1) < 64

    for i in range(1, NX):
        arrive(meta.at[(x + NX - i) % NX], m_ss.at[i], m_rs.at[i], xpeer(i))
    info = jnp.concatenate(
        [jnp.where(low, meta[b], pltpu.roll(meta[b + 1], 64, 1)) for b in (0, 2)], axis=1
    )
    named = jnp.zeros(shape, f32)
    scale = jnp.zeros(shape, f32)
    for k in range(8):
        hit = info[k : k + 1, :] == expert
        named = named + jnp.where(hit, f32(1), f32(0))
        scale = scale + jnp.where(hit, info[8 + k : 9 + k, :], f32(0))
    rank = jnp.dot(named.astype(bf16), before, preferred_element_type=f32)
    rank = jnp.where(named > 0, rank, f32(-1)).reshape(NZ, 1, 8, NX * rows_n)

    def chosen(first, last):
        shape = (last - first, CAP, 8, NX * rows_n)
        place = lax.broadcasted_iota(jnp.int32, shape, 1).astype(f32)
        return jnp.broadcast_to(rank[first:last], shape) == place

    for i in range(1, NX):
        arrive(tx.at[(x + NX - i) % NX], x_ss.at[i], x_rs.at[i], xpeer(i))
    block = tx[...].reshape(NX * rows_n, feats)

    def step_out(g):
        pick = jnp.where(chosen(STARTS[g], STARTS[g + 1]), f32(1), f32(0))
        pick = pick.reshape((STARTS[g + 1] - STARTS[g]) * SLOT, NX * rows_n).astype(bf16)
        send[group(g), :] = jnp.dot(pick, block, preferred_element_type=f32).astype(bf16)
        for s in range(STARTS[g], STARTS[g + 1]):
            part = pl.ds(s * SLOT, SLOT)
            if s == OWN:
                gath[d, part, :] = send[part, :]
            else:
                go(send.at[part, :], gath.at[d, part, :], z_ss.at[s], z_rs.at[s], zpeer(offset(s)))

    for g in range(AHEAD):
        step_out(g)
    scale = jnp.broadcast_to(scale.reshape(NZ, 1, 8, NX * rows_n), (NZ, CAP, 8, NX * rows_n))
    mix = jnp.where(chosen(0, NZ), scale, f32(0)).reshape(NZ * SLOT, NX * rows_n)
    comb[...] = mix.astype(bf16)

    def half(g):
        return ((STARTS[g + 1] - STARTS[g]) * SLOT // 2 + 15) // 16 * 16

    def first(g):
        return pl.ds(STARTS[g] * SLOT, half(g))

    def second(g):
        return pl.ds(STARTS[g] * SLOT + half(g), (STARTS[g + 1] - STARTS[g]) * SLOT - half(g))

    def step_own(g):
        for s in [i for i in range(STARTS[g], STARTS[g + 1]) if i != OWN]:
            arrive(gath.at[d, pl.ds(s * SLOT, SLOT), :], z_ss.at[s], z_rs.at[s], zpeer(offset(s)))
        if g + AHEAD < GROUPS:
            step_out(g + AHEAD)
        mine = gath.at[d, group(g), :]
        go(mine, mine, ag_ss.at[g, 0], ag_rs.at[g, 0], right)
        go(mine, mine, ag_ss.at[g, 1], ag_rs.at[g, 1], left)
        if DIRECT[g]:
            go(mine, mine, ag_ss.at[g, 3], ag_rs.at[g, 3], across)
        go(mine, mine, ag_ss.at[g, 2], ag_rs.at[g, 2], sibling)

    def step_forward(g):
        from_l, from_r = yl * 2 + c, yr * 2 + c
        arrive(gath.at[from_l, group(g), :], ag_ss.at[g, 0], ag_rs.at[g, 0], right)
        if not DIRECT[g]:
            part = gath.at[from_l, first(g), :]
            go(part, part, ag_ss.at[g, 3], ag_rs.at[g, 3], right)
        arrive(gath.at[from_r, group(g), :], ag_ss.at[g, 1], ag_rs.at[g, 1], left)
        if not DIRECT[g]:
            part = gath.at[from_r, second(g), :]
            go(part, part, ag_ss.at[g, 4], ag_rs.at[g, 4], left)
        part = gath.at[from_l, group(g), :]
        go(part, part, ag_ss.at[g, 5], ag_rs.at[g, 5], sibling)
        part = gath.at[from_r, group(g), :]
        go(part, part, ag_ss.at[g, 6], ag_rs.at[g, 6], sibling)

    def step_last(g):
        other = yo * 2 + c
        if DIRECT[g]:
            arrive(gath.at[other, group(g), :], ag_ss.at[g, 3], ag_rs.at[g, 3], across)
        else:
            arrive(gath.at[other, first(g), :], ag_ss.at[g, 3], ag_rs.at[g, 3], right)
            arrive(gath.at[other, second(g), :], ag_ss.at[g, 4], ag_rs.at[g, 4], left)
        part = gath.at[other, group(g), :]
        go(part, part, ag_ss.at[g, 7], ag_rs.at[g, 7], sibling)

    def step_experts(g):
        for i, yy in ((2, y), (5, yl), (6, yr), (7, yo)):
            arrive(gath.at[yy * 2 + 1 - c, group(g), :], ag_ss.at[g, i], ag_rs.at[g, i], sibling)
        if not ready:
            ready.append(True)
            for copy in weights:
                copy.wait()
        lhs = jnp.concatenate([gath[i, group(g), :] for i in range(2 * NY)], axis=1)
        both = jnp.dot(lhs, wgu[...], preferred_element_type=f32)
        gate, up = both[:, 0:256], both[:, 256:512]
        hidden = gate / (f32(1) + jnp.exp(-gate)) * up
        r = lax.broadcasted_iota(jnp.int32, hidden.shape, 0)
        lane = lax.broadcasted_iota(jnp.int32, hidden.shape, 1)
        hidden = jnp.where((r & 1) == (lane >> 7), hidden, f32(0)).astype(bf16)
        for yy in range(NY):
            cols = pl.ds(pl.multiple_of((2 * yy + 1 - c) * feats, feats), feats)
            psib[yy, group(g), :] = jnp.dot(hidden, wdn[:, cols], preferred_element_type=f32).astype(bf16)
        go(psib.at[:, group(g), :], sib.at[:, group(g), :], rs_ss.at[g, 0], rs_rs.at[g, 0], sibling)
        for yy in range(NY):
            cols = pl.ds(pl.multiple_of((2 * yy + c) * feats, feats), feats)
            own[yy, group(g), :] = jnp.dot(hidden, wdn[:, cols], preferred_element_type=f32)

    def step_pair(g):
        arrive(sib.at[:, group(g), :], rs_ss.at[g, 0], rs_rs.at[g, 0], sibling)
        for yy in range(NY):
            total = own[yy, group(g), :] + sib[yy, group(g), :].astype(f32)
            uni[yy, group(g), :] = total.astype(bf16)
        if DIRECT[g]:
            go(uni.at[yo, group(g), :], far.at[group(g), :], rs_ss.at[g, 1], rs_rs.at[g, 1], across)
            go(uni.at[yr, group(g), :], fl.at[group(g), :], rs_ss.at[g, 3], rs_rs.at[g, 3], right)
            go(uni.at[yl, group(g), :], fr.at[group(g), :], rs_ss.at[g, 4], rs_rs.at[g, 4], left)
        else:
            go(uni.at[yo, first(g), :], far.at[first(g), :], rs_ss.at[g, 1], rs_rs.at[g, 1], right)
            go(uni.at[yo, second(g), :], far.at[second(g), :], rs_ss.at[g, 2], rs_rs.at[g, 2], left)

    def step_near(g):
        if DIRECT[g]:
            return
        arrive(far.at[first(g), :], rs_ss.at[g, 1], rs_rs.at[g, 1], right)
        total = uni[yr, first(g), :].astype(f32) + far[first(g), :].astype(f32)
        uni[yr, first(g), :] = total.astype(bf16)
        go(uni.at[yr, group(g), :], fl.at[group(g), :], rs_ss.at[g, 3], rs_rs.at[g, 3], right)
        arrive(far.at[second(g), :], rs_ss.at[g, 2], rs_rs.at[g, 2], left)
        total = uni[yl, second(g), :].astype(f32) + far[second(g), :].astype(f32)
        uni[yl, second(g), :] = total.astype(bf16)
        go(uni.at[yl, group(g), :], fr.at[group(g), :], rs_ss.at[g, 4], rs_rs.at[g, 4], left)

    def step_back(g):
        arrive(fl.at[group(g), :], rs_ss.at[g, 3], rs_rs.at[g, 3], right)
        arrive(fr.at[group(g), :], rs_ss.at[g, 4], rs_rs.at[g, 4], left)
        total = uni[y, group(g), :].astype(f32) + fl[group(g), :].astype(f32) + fr[group(g), :].astype(f32)
        if DIRECT[g]:
            arrive(far.at[group(g), :], rs_ss.at[g, 1], rs_rs.at[g, 1], across)
            total = total + far[group(g), :].astype(f32)
        total = total.astype(bf16)
        fin[group(g), :] = total
        for s in [i for i in range(STARTS[g], STARTS[g + 1]) if i != OWN]:
            part = pl.ds(s * SLOT, SLOT)
            go(fin.at[part, :], ret.at[part, :], zr_ss.at[s], zr_rs.at[s], zpeer(NZ - offset(s)))
        if STARTS[g] <= OWN < STARTS[g + 1]:
            ret[OWN * SLOT : (OWN + 1) * SLOT, :] = fin[OWN * SLOT : (OWN + 1) * SLOT, :]

    def step_mix(g):
        for s in [i for i in range(STARTS[g], STARTS[g + 1]) if i != OWN]:
            part = pl.ds(s * SLOT, SLOT)
            arrive(ret.at[part, :], zr_ss.at[s], zr_rs.at[s], zpeer(NZ - offset(s)))
        acc[...] += lax.dot_general(
            comb[group(g), :], ret[group(g), :], (((0,), (0,)), ((), ())), preferred_element_type=f32
        )

    steps = [step_own, step_forward, step_last, step_experts, step_pair, step_near, step_back, step_mix]
    for k, g in ORDER:
        steps[k](g)

    xout[...] = acc[...].astype(bf16).reshape(NX, rows_n, feats)
    for i in range(1, NX):
        go(xout.at[(x + i) % NX], xin.at[i], xr_ss.at[i], xr_rs.at[i], xpeer(i))
    total = acc[pl.ds(pl.multiple_of(x * rows_n, rows_n), rows_n), :]
    for copy in sent[: 1 - NX]:
        copy.wait_send()
    for i in range(1, NX):
        arrive(xin.at[i], xr_ss.at[i], xr_rs.at[i], xpeer(i))
        total = total + xin[i].astype(f32)
    out_ref[...] = total.astype(bf16)
    for copy in sent[1 - NX :]:
        copy.wait_send()


def on_device(tokens, expert_ids, route_weights, w_gate, w_up, w_down):
    rows_n, feats = tokens.shape
    vm, dma = pltpu.VMEM, pltpu.SemaphoreType.DMA
    bf16, f32 = jnp.bfloat16, jnp.float32
    total = NZ * SLOT
    width = w_gate.shape[1]
    in_vmem = pl.BlockSpec(memory_space=pltpu.VMEM)
    in_hbm = pl.BlockSpec(memory_space=pltpu.HBM)
    return pl.pallas_call(
        kernel,
        out_shape=jax.ShapeDtypeStruct((rows_n, feats), bf16),
        in_specs=[in_hbm] * 6,
        out_specs=in_vmem,
        scratch_shapes=[
            vm((NX, rows_n, feats), bf16),
            vm((8, rows_n), jnp.int32),
            vm((8, rows_n), bf16),
            vm((NX, 16, 128), f32),
            vm((total, feats), bf16),
            vm((2 * NY, total, feats), bf16),
            vm((width, 512), bf16),
            vm((256, width), bf16),
            vm((total, NX * rows_n), bf16),
            vm((NY, total, feats), bf16),
            vm((NY, total, feats), f32),
            vm((NY, total, feats), bf16),
            vm((NY, total, feats), bf16),
            vm((total, feats), bf16),
            vm((total, feats), bf16),
            vm((total, feats), bf16),
            vm((total, feats), bf16),
            vm((total, feats), bf16),
            vm((NX * rows_n, feats), f32),
            vm((NX, rows_n, feats), bf16),
            vm((NX, rows_n, feats), bf16),
            dma((NX,)), dma((NX,)), dma((NX,)), dma((NX,)),
            dma((NZ,)), dma((NZ,)),
            dma((GROUPS, 8)), dma((GROUPS, 8)),
            dma((GROUPS, 5)), dma((GROUPS, 5)),
            dma((NZ,)), dma((NZ,)),
            dma((NX,)), dma((NX,)),
            dma((9,)),
        ],
        compiler_params=pltpu.CompilerParams(
            collective_id=0, has_side_effects=True, vmem_limit_bytes=60 << 20
        ),
    )(tokens, expert_ids.T, route_weights.T, w_gate, w_up, w_down)


def solution(mesh):
    return jax.shard_map(
        on_device,
        mesh=mesh,
        in_specs=(
            P("expert", "dp"),
            P("expert", None),
            P("expert", None),
            P("expert", None, "dp"),
            P("expert", None, "dp"),
            P("expert", "dp", None),
        ),
        out_specs=P("expert", "dp"),
        check_vma=False,
    )
```

```python
import functools

import jax
import jax.numpy as jnp
from jax import lax
from jax.experimental import pallas as pl
from jax.experimental.pallas import tpu as pltpu
from jax.sharding import PartitionSpec as P

MESH = pl.DeviceIdType.MESH
NX, NY, NZ = 4, 4, 16
CAP = 6
SLOT = NX * 2 * CAP
GROUPS = 7
STARTS = (0, 2, 4, 6, 8, 10, 12, 16)
OFFSETS = (6, 10, 5, 11, 0, 8, 3, 13, 4, 12, 7, 9, 2, 14, 1, 15)
DIRECT = (True, False, False, False, False, True, False)
OWN = 4
AHEAD = 4
ORDER = (
    (0, 0), (0, 1), (1, 0), (0, 3), (2, 0), (1, 1), (0, 2), (3, 0),
    (0, 4), (4, 0), (5, 0), (1, 3), (2, 1), (1, 2), (3, 1), (1, 4),
    (4, 1), (0, 6), (0, 5), (2, 3), (6, 0), (2, 2), (2, 4), (3, 3),
    (5, 1), (3, 2), (3, 4), (4, 3), (4, 2), (1, 6), (4, 4), (1, 5),
    (2, 5), (6, 1), (5, 3), (3, 5), (5, 2), (2, 6), (4, 5), (5, 5),
    (5, 4), (3, 6), (6, 3), (6, 2), (4, 6), (6, 5), (6, 4), (5, 6),
    (6, 6), (7, 0), (7, 1), (7, 3), (7, 2), (7, 5), (7, 4), (7, 6),
)


def kernel(
    tok_ref, ids_ref, rw_ref, wg_ref, wu_ref, wd_ref, out_ref,
    tx, ids_v, rw_v, meta, send, gath, wgu, wdn, comb, psib, own, sib, uni, far, fl, fr, fin, ret, acc, xout, xin,
    x_ss, x_rs, m_ss, m_rs, z_ss, z_rs, ag_ss, ag_rs, rs_ss, rs_rs, zr_ss, zr_rs, xr_ss, xr_rs, w_sem,
):
    f32, bf16 = jnp.float32, jnp.bfloat16
    rows_n, feats = tok_ref.shape
    d, ex = lax.axis_index("dp"), lax.axis_index("expert")
    y, c = d // 2, d % 2
    x, z = ex // NZ, ex % NZ
    yr, yl, yo = (y + 1) % NY, (y + NY - 1) % NY, (y + 2) % NY
    right, left, across = (yr * 2 + c, ex), (yl * 2 + c, ex), (yo * 2 + c, ex)
    sibling = (y * 2 + 1 - c, ex)

    def xpeer(i):
        return (d, ((x + i) % NX) * NZ + z)

    def zpeer(o):
        return (d, x * NZ + (z + o) % NZ)

    def offset(s):
        return OFFSETS[s]

    def remote(src, dst, ss, rs, dev):
        return pltpu.make_async_remote_copy(
            src_ref=src, dst_ref=dst, send_sem=ss, recv_sem=rs, device_id=dev, device_id_type=MESH
        )

    sent, ready = [], []

    def go(src, dst, ss, rs, dev):
        copy = remote(src, dst, ss, rs, dev)
        copy.start()
        sent.append(copy)

    def arrive(dst, ss, rs, dev):
        remote(dst, dst, ss, rs, dev).wait_recv()

    def group(g):
        return pl.ds(STARTS[g] * SLOT, (STARTS[g + 1] - STARTS[g]) * SLOT)

    barrier = pltpu.get_barrier_semaphore()
    partners = [xpeer(i) for i in range(1, NX)] + [zpeer(o) for o in range(1, NZ)] + [right, left, across, sibling]
    for dev in partners:
        pl.semaphore_signal(barrier, inc=1, device_id=dev, device_id_type=MESH)

    x_in = [
        pltpu.make_async_copy(ids_ref, ids_v, w_sem.at[6]),
        pltpu.make_async_copy(rw_ref, rw_v, w_sem.at[7]),
        pltpu.make_async_copy(tok_ref, tx.at[x], w_sem.at[8]),
    ]
    for copy in x_in:
        copy.start()
    weights = [
        pltpu.make_async_copy(wg_ref.at[0], wgu.at[:, 0:128], w_sem.at[0]),
        pltpu.make_async_copy(wg_ref.at[1], wgu.at[:, 128:256], w_sem.at[1]),
        pltpu.make_async_copy(wu_ref.at[0], wgu.at[:, 256:384], w_sem.at[2]),
        pltpu.make_async_copy(wu_ref.at[1], wgu.at[:, 384:512], w_sem.at[3]),
        pltpu.make_async_copy(wd_ref.at[0], wdn.at[0:128, :], w_sem.at[4]),
        pltpu.make_async_copy(wd_ref.at[1], wdn.at[128:256, :], w_sem.at[5]),
    ]
    for copy in weights:
        copy.start()

    meta[x] = jnp.zeros((16, 128), f32)
    acc[...] = jnp.zeros(acc.shape, f32)
    for copy in x_in:
        copy.wait()
    meta[x, 0:8, 0:64] = ids_v[...].astype(f32)
    meta[x, 8:16, 0:64] = rw_v[...].astype(f32)
    pl.semaphore_wait(barrier, len(partners))

    for i in range(1, NX):
        go(meta.at[x], meta.at[x], m_ss.at[i], m_rs.at[i], xpeer(i))
    for i in range(1, NX):
        go(tx.at[x], tx.at[x], x_ss.at[i], x_rs.at[i], xpeer(i))

    shape = (NZ * 8, NX * rows_n)
    q = lax.broadcasted_iota(jnp.int32, shape, 0)
    t = lax.broadcasted_iota(jnp.int32, shape, 1)
    s = q >> 3
    off = jnp.zeros(shape, jnp.int32)
    for i in range(NZ):
        off = jnp.where(s == i, OFFSETS[i], off)
    expert = 2 * (x * NZ + ((z + off) & (NZ - 1))) + (q & 1)
    expert = jnp.where(((q >> 1) & (NX - 1)) == (t >> 6), expert, -1).astype(f32)
    t0 = lax.broadcasted_iota(jnp.int32, (NX * rows_n, NX * rows_n), 0)
    t1 = lax.broadcasted_iota(jnp.int32, (NX * rows_n, NX * rows_n), 1)
    before = jnp.where((t0 < t1) & ((t0 >> 6) == (t1 >> 6)), f32(1), f32(0)).astype(bf16)
    low = lax.broadcasted_iota(jnp.int32, (16, 128), 1) < 64

    for i in range(1, NX):
        arrive(meta.at[(x + NX - i) % NX], m_ss.at[i], m_rs.at[i], xpeer(i))
    info = jnp.concatenate(
        [jnp.where(low, meta[b], pltpu.roll(meta[b + 1], 64, 1)) for b in (0, 2)], axis=1
    )
    named = jnp.zeros(shape, f32)
    scale = jnp.zeros(shape, f32)
    for k in range(8):
        hit = info[k : k + 1, :] == expert
        named = named + jnp.where(hit, f32(1), f32(0))
        scale = scale + jnp.where(hit, info[8 + k : 9 + k, :], f32(0))
    rank = jnp.dot(named.astype(bf16), before, preferred_element_type=f32)
    rank = jnp.where(named > 0, rank, f32(-1)).reshape(NZ, 1, 8, NX * rows_n)

    def chosen(first, last):
        shape = (last - first, CAP, 8, NX * rows_n)
        place = lax.broadcasted_iota(jnp.int32, shape, 1).astype(f32)
        return jnp.broadcast_to(rank[first:last], shape) == place

    for i in range(1, NX):
        arrive(tx.at[(x + NX - i) % NX], x_ss.at[i], x_rs.at[i], xpeer(i))
    block = tx[...].reshape(NX * rows_n, feats)

    def step_out(g):
        pick = jnp.where(chosen(STARTS[g], STARTS[g + 1]), f32(1), f32(0))
        pick = pick.reshape((STARTS[g + 1] - STARTS[g]) * SLOT, NX * rows_n).astype(bf16)
        send[group(g), :] = jnp.dot(pick, block, preferred_element_type=f32).astype(bf16)
        for s in range(STARTS[g], STARTS[g + 1]):
            part = pl.ds(s * SLOT, SLOT)
            if s == OWN:
                gath[d, part, :] = send[part, :]
            else:
                go(send.at[part, :], gath.at[d, part, :], z_ss.at[s], z_rs.at[s], zpeer(offset(s)))

    for g in range(AHEAD):
        step_out(g)
    scale = jnp.broadcast_to(scale.reshape(NZ, 1, 8, NX * rows_n), (NZ, CAP, 8, NX * rows_n))
    mix = jnp.where(chosen(0, NZ), scale, f32(0)).reshape(NZ * SLOT, NX * rows_n)
    comb[...] = mix.astype(bf16)

    def half(g):
        return ((STARTS[g + 1] - STARTS[g]) * SLOT // 2 + 15) // 16 * 16

    def first(g):
        return pl.ds(STARTS[g] * SLOT, half(g))

    def second(g):
        return pl.ds(STARTS[g] * SLOT + half(g), (STARTS[g + 1] - STARTS[g]) * SLOT - half(g))

    def step_own(g):
        for s in [i for i in range(STARTS[g], STARTS[g + 1]) if i != OWN]:
            arrive(gath.at[d, pl.ds(s * SLOT, SLOT), :], z_ss.at[s], z_rs.at[s], zpeer(offset(s)))
        if g + AHEAD < GROUPS:
            step_out(g + AHEAD)
        mine = gath.at[d, group(g), :]
        go(mine, mine, ag_ss.at[g, 0], ag_rs.at[g, 0], right)
        go(mine, mine, ag_ss.at[g, 1], ag_rs.at[g, 1], left)
        if DIRECT[g]:
            go(mine, mine, ag_ss.at[g, 3], ag_rs.at[g, 3], across)
        go(mine, mine, ag_ss.at[g, 2], ag_rs.at[g, 2], sibling)

    def step_forward(g):
        from_l, from_r = yl * 2 + c, yr * 2 + c
        arrive(gath.at[from_l, group(g), :], ag_ss.at[g, 0], ag_rs.at[g, 0], right)
        if not DIRECT[g]:
            part = gath.at[from_l, first(g), :]
            go(part, part, ag_ss.at[g, 3], ag_rs.at[g, 3], right)
        arrive(gath.at[from_r, group(g), :], ag_ss.at[g, 1], ag_rs.at[g, 1], left)
        if not DIRECT[g]:
            part = gath.at[from_r, second(g), :]
            go(part, part, ag_ss.at[g, 4], ag_rs.at[g, 4], left)
        part = gath.at[from_l, group(g), :]
        go(part, part, ag_ss.at[g, 5], ag_rs.at[g, 5], sibling)
        part = gath.at[from_r, group(g), :]
        go(part, part, ag_ss.at[g, 6], ag_rs.at[g, 6], sibling)

    def step_last(g):
        other = yo * 2 + c
        if DIRECT[g]:
            arrive(gath.at[other, group(g), :], ag_ss.at[g, 3], ag_rs.at[g, 3], across)
        else:
            arrive(gath.at[other, first(g), :], ag_ss.at[g, 3], ag_rs.at[g, 3], right)
            arrive(gath.at[other, second(g), :], ag_ss.at[g, 4], ag_rs.at[g, 4], left)
        part = gath.at[other, group(g), :]
        go(part, part, ag_ss.at[g, 7], ag_rs.at[g, 7], sibling)

    def step_experts(g):
        for i, yy in ((2, y), (5, yl), (6, yr), (7, yo)):
            arrive(gath.at[yy * 2 + 1 - c, group(g), :], ag_ss.at[g, i], ag_rs.at[g, i], sibling)
        if not ready:
            ready.append(True)
            for copy in weights:
                copy.wait()
        lhs = jnp.concatenate([gath[i, group(g), :] for i in range(2 * NY)], axis=1)
        both = jnp.dot(lhs, wgu[...], preferred_element_type=f32)
        gate, up = both[:, 0:256], both[:, 256:512]
        hidden = gate / (f32(1) + jnp.exp(-gate)) * up
        r = lax.broadcasted_iota(jnp.int32, hidden.shape, 0)
        lane = lax.broadcasted_iota(jnp.int32, hidden.shape, 1)
        hidden = jnp.where((r & 1) == (lane >> 7), hidden, f32(0)).astype(bf16)
        for yy in range(NY):
            cols = pl.ds(pl.multiple_of((2 * yy + 1 - c) * feats, feats), feats)
            psib[yy, group(g), :] = jnp.dot(hidden, wdn[:, cols], preferred_element_type=f32).astype(bf16)
        go(psib.at[:, group(g), :], sib.at[:, group(g), :], rs_ss.at[g, 0], rs_rs.at[g, 0], sibling)
        for yy in range(NY):
            cols = pl.ds(pl.multiple_of((2 * yy + c) * feats, feats), feats)
            own[yy, group(g), :] = jnp.dot(hidden, wdn[:, cols], preferred_element_type=f32)

    def step_pair(g):
        arrive(sib.at[:, group(g), :], rs_ss.at[g, 0], rs_rs.at[g, 0], sibling)
        for yy in range(NY):
            total = own[yy, group(g), :] + sib[yy, group(g), :].astype(f32)
            uni[yy, group(g), :] = total.astype(bf16)
        if DIRECT[g]:
            go(uni.at[yo, group(g), :], far.at[group(g), :], rs_ss.at[g, 1], rs_rs.at[g, 1], across)
            go(uni.at[yr, group(g), :], fl.at[group(g), :], rs_ss.at[g, 3], rs_rs.at[g, 3], right)
            go(uni.at[yl, group(g), :], fr.at[group(g), :], rs_ss.at[g, 4], rs_rs.at[g, 4], left)
        else:
            go(uni.at[yo, first(g), :], far.at[first(g), :], rs_ss.at[g, 1], rs_rs.at[g, 1], right)
            go(uni.at[yo, second(g), :], far.at[second(g), :], rs_ss.at[g, 2], rs_rs.at[g, 2], left)

    def step_near(g):
        if DIRECT[g]:
            return
        arrive(far.at[first(g), :], rs_ss.at[g, 1], rs_rs.at[g, 1], right)
        total = uni[yr, first(g), :].astype(f32) + far[first(g), :].astype(f32)
        uni[yr, first(g), :] = total.astype(bf16)
        go(uni.at[yr, group(g), :], fl.at[group(g), :], rs_ss.at[g, 3], rs_rs.at[g, 3], right)
        arrive(far.at[second(g), :], rs_ss.at[g, 2], rs_rs.at[g, 2], left)
        total = uni[yl, second(g), :].astype(f32) + far[second(g), :].astype(f32)
        uni[yl, second(g), :] = total.astype(bf16)
        go(uni.at[yl, group(g), :], fr.at[group(g), :], rs_ss.at[g, 4], rs_rs.at[g, 4], left)

    def step_back(g):
        arrive(fl.at[group(g), :], rs_ss.at[g, 3], rs_rs.at[g, 3], right)
        arrive(fr.at[group(g), :], rs_ss.at[g, 4], rs_rs.at[g, 4], left)
        total = uni[y, group(g), :].astype(f32) + fl[group(g), :].astype(f32) + fr[group(g), :].astype(f32)
        if DIRECT[g]:
            arrive(far.at[group(g), :], rs_ss.at[g, 1], rs_rs.at[g, 1], across)
            total = total + far[group(g), :].astype(f32)
        total = total.astype(bf16)
        fin[group(g), :] = total
        for s in [i for i in range(STARTS[g], STARTS[g + 1]) if i != OWN]:
            part = pl.ds(s * SLOT, SLOT)
            go(fin.at[part, :], ret.at[part, :], zr_ss.at[s], zr_rs.at[s], zpeer(NZ - offset(s)))
        if STARTS[g] <= OWN < STARTS[g + 1]:
            ret[OWN * SLOT : (OWN + 1) * SLOT, :] = fin[OWN * SLOT : (OWN + 1) * SLOT, :]

    def step_mix(g):
        for s in [i for i in range(STARTS[g], STARTS[g + 1]) if i != OWN]:
            part = pl.ds(s * SLOT, SLOT)
            arrive(ret.at[part, :], zr_ss.at[s], zr_rs.at[s], zpeer(NZ - offset(s)))
        acc[...] += lax.dot_general(
            comb[group(g), :], ret[group(g), :], (((0,), (0,)), ((), ())), preferred_element_type=f32
        )

    steps = [step_own, step_forward, step_last, step_experts, step_pair, step_near, step_back, step_mix]
    for k, g in ORDER:
        steps[k](g)

    xout[...] = acc[...].astype(bf16).reshape(NX, rows_n, feats)
    for i in range(1, NX):
        go(xout.at[(x + i) % NX], xin.at[i], xr_ss.at[i], xr_rs.at[i], xpeer(i))
    total = acc[pl.ds(pl.multiple_of(x * rows_n, rows_n), rows_n), :]
    for copy in sent[: 1 - NX]:
        copy.wait_send()
    for i in range(1, NX):
        arrive(xin.at[i], xr_ss.at[i], xr_rs.at[i], xpeer(i))
        total = total + xin[i].astype(f32)
    out_ref[...] = total.astype(bf16)
    for copy in sent[1 - NX :]:
        copy.wait_send()


def on_device(tokens, expert_ids, route_weights, w_gate, w_up, w_down):
    rows_n, feats = tokens.shape
    vm, dma = pltpu.VMEM, pltpu.SemaphoreType.DMA
    bf16, f32 = jnp.bfloat16, jnp.float32
    total = NZ * SLOT
    width = w_gate.shape[1]
    in_vmem = pl.BlockSpec(memory_space=pltpu.VMEM)
    in_hbm = pl.BlockSpec(memory_space=pltpu.HBM)
    return pl.pallas_call(
        kernel,
        out_shape=jax.ShapeDtypeStruct((rows_n, feats), bf16),
        in_specs=[in_hbm] * 6,
        out_specs=in_vmem,
        scratch_shapes=[
            vm((NX, rows_n, feats), bf16),
            vm((8, rows_n), jnp.int32),
            vm((8, rows_n), bf16),
            vm((NX, 16, 128), f32),
            vm((total, feats), bf16),
            vm((2 * NY, total, feats), bf16),
            vm((width, 512), bf16),
            vm((256, width), bf16),
            vm((total, NX * rows_n), bf16),
            vm((NY, total, feats), bf16),
            vm((NY, total, feats), f32),
            vm((NY, total, feats), bf16),
            vm((NY, total, feats), bf16),
            vm((total, feats), bf16),
            vm((total, feats), bf16),
            vm((total, feats), bf16),
            vm((total, feats), bf16),
            vm((total, feats), bf16),
            vm((NX * rows_n, feats), f32),
            vm((NX, rows_n, feats), bf16),
            vm((NX, rows_n, feats), bf16),
            dma((NX,)), dma((NX,)), dma((NX,)), dma((NX,)),
            dma((NZ,)), dma((NZ,)),
            dma((GROUPS, 8)), dma((GROUPS, 8)),
            dma((GROUPS, 5)), dma((GROUPS, 5)),
            dma((NZ,)), dma((NZ,)),
            dma((NX,)), dma((NX,)),
            dma((9,)),
        ],
        compiler_params=pltpu.CompilerParams(
            collective_id=0, has_side_effects=True, vmem_limit_bytes=60 << 20
        ),
    )(tokens, expert_ids.T, route_weights.T, w_gate, w_up, w_down)


def solution(mesh):
    return jax.shard_map(
        on_device,
        mesh=mesh,
        in_specs=(
            P("expert", "dp"),
            P("expert", None),
            P("expert", None),
            P("expert", None, "dp"),
            P("expert", None, "dp"),
            P("expert", "dp", None),
        ),
        out_specs=P("expert", "dp"),
        check_vma=False,
    )
```
